32 devices in a mesh: replica: 8 (over z, y), shard: 4 (over x, core).
Axes of the slice: x: 2, y: 2, z: 4, core: 2. Of those that a mesh axis runs over, the one named last changes fastest.
Arguments:
- tokens: bfloat16 [16, 256, 1152], P('replica', 'shard'), may hold values from -6 to 6
- positions: int32 [16, 256], P('replica', 'shard'), may hold values from 0 to 255, as said below
- cotangent: bfloat16 [16, 256, 1152], P('replica', 'shard'), may hold values from -6 to 6
- live_count: int32 [8], P('replica'), may hold values from 1 to 2, as said below
- qkv_weight: bfloat16 [1152, 1536], P('shard'), may hold values from -0.1875 to 0.1875
- out_weight: bfloat16 [1024, 1152], P('shard'), may hold values from -0.1875 to 0.1875
- gate_weight: bfloat16 [1152, 6912], P('shard'), may hold values from -0.1875 to 0.1875
- up_weight: bfloat16 [1152, 6912], P('shard'), may hold values from -0.1875 to 0.1875
- down_weight: bfloat16 [6912, 1152], P('shard'), may hold values from -0.078125 to 0.078125
- gain_in: float32 [1152], replicated, may hold values from 0.25 to 1.75
- gain_query: float32 [256], replicated, may hold values from 0.25 to 1.75
- gain_key: float32 [256], replicated, may hold values from 0.25 to 1.75
- gain_attn: float32 [1152], replicated, may hold values from 0.25 to 1.75
- gain_pre: float32 [1152], replicated, may hold values from 0.25 to 1.75
- gain_post: float32 [1152], replicated, may hold values from 0.25 to 1.75
Outputs:
- output: float32 [16, 256, 1152], P('replica', 'shard')
- input_grad: float32 [16, 256, 1152], P('replica', 'shard')
- qkv_grad: float32 [1152, 1536], P('shard', 'replica')
- out_grad: float32 [1024, 1152], P('shard', 'replica')
- gate_grad: float32 [1152, 6912], P('shard', 'replica')
- up_grad: float32 [1152, 6912], P('shard', 'replica')
- down_grad: float32 [6912, 1152], P('shard', 'replica')
- gain_in_grad: float32 [1152], replicated
- gain_query_grad: float32 [256], replicated
- gain_key_grad: float32 [256], replicated
- gain_attn_grad: float32 [1152], replicated
- gain_pre_grad: float32 [1152], replicated
- gain_post_grad: float32 [1152], replicated
The draws below stay inside these ranges and needn't reach their ends.
Inputs may be any that keep to these rules, and one draw needn't show every extreme that they name: Each sequence holds one or two documents whose positions count from 0 by one; some sequence is a single document of 256 tokens. `live_count`: some group has all 2 slots live.
All inputs are finite; a program needn't handle non-finite values.
Results may differ from the reference program's by a relative error of at most 0.015.
Values may be sent and summed in bfloat16 or wider, within the bound.
No kernel may reach another device: no remote copies, remote signals or barrier semaphores. Data moves between devices by JAX's collectives and lax.ppermute only.
A program may use at most 192 MiB of HBM per device.

```python
import math
import jax
import jax.numpy as jnp
from jax import lax

D = 1152
H = 4
HD = 256
FF = 6912
LEN = 256
SLOTS = 2
GROUPS = 8
NSEQ = 16


def draw_positions(key, part):
    cuts = jax.random.randint(key, (NSEQ, 1), 0, LEN)
    cuts = cuts.at[0, 0].set(0)
    seq_index = jnp.arange(LEN, dtype=jnp.int32)[None, :]
    return jnp.where(seq_index >= cuts, seq_index - cuts, seq_index).astype(jnp.int32)


def draw_live_count(key, part):
    counts = jax.random.randint(key, (GROUPS,), 1, SLOTS + 1)
    full_group = jax.random.randint(jax.random.fold_in(key, 7), (), 0, GROUPS)
    return jnp.where(jnp.arange(GROUPS) == full_group, SLOTS, counts).astype(jnp.int32)


def block_levels(stream_key, extent, shards, smallest, top_value):
    factor_of, own = 1.0, jax.random.fold_in(stream_key, 6)
    for dim, blocks in shards:
        heights = jnp.exp(jax.random.uniform(jax.random.fold_in(own, dim), (blocks,), jnp.float32, smallest / len(shards), top_value / len(shards)))
        factor_of = factor_of * jnp.repeat(heights, extent[dim] // blocks).reshape([-1 if axis == dim else 1 for axis in range(len(extent))])
    return factor_of


def gaussian(stream_key, dims, spread, most, shards=(), kind=jnp.bfloat16):
    entries = spread * jax.random.normal(stream_key, dims, jnp.float32)
    if shards:
        entries = entries * block_levels(stream_key, dims, shards, -0.22, 0.18)
    return jnp.clip(entries, -most, most).astype(kind)


def setup_inputs(seed: int = 0) -> dict:
    streams_of = jax.random.split(jax.random.key(seed), 16)
    tokens = gaussian(streams_of[0], (NSEQ, LEN, D), 1.0, 6.0, ((0, 8), (1, 4)))
    positions = draw_positions(jax.random.fold_in(streams_of[15], 71), 0)
    cotangent = gaussian(streams_of[2], (NSEQ, LEN, D), 1.0, 6.0, ((0, 8), (1, 4)))
    live_count = draw_live_count(jax.random.fold_in(streams_of[15], 71), 0)
    qkv_weight = gaussian(streams_of[4], (D, (H + 2) * HD), D ** -0.5, 0.1875, ((0, 4),))
    out_weight = gaussian(streams_of[5], (H * HD, D), (H * HD) ** -0.5, 0.1875, ((0, 4),))
    gate_weight = gaussian(streams_of[6], (D, FF), D ** -0.5, 0.1875, ((0, 4),))
    up_weight = gaussian(streams_of[7], (D, FF), D ** -0.5, 0.1875, ((0, 4),))
    down_weight = gaussian(streams_of[8], (FF, D), FF ** -0.5, 0.078125, ((0, 4),))
    gain_in = jnp.clip(1.0 + 0.15 * jax.random.normal(streams_of[9], (D,), jnp.float32), 0.25, 1.75)
    gain_query = jnp.clip(1.0 + 0.15 * jax.random.normal(streams_of[10], (HD,), jnp.float32), 0.25, 1.75)
    gain_key = jnp.clip(1.0 + 0.15 * jax.random.normal(streams_of[11], (HD,), jnp.float32), 0.25, 1.75)
    gain_attn = jnp.clip(1.0 + 0.15 * jax.random.normal(streams_of[12], (D,), jnp.float32), 0.25, 1.75)
    gain_pre = jnp.clip(1.0 + 0.15 * jax.random.normal(streams_of[13], (D,), jnp.float32), 0.25, 1.75)
    gain_post = jnp.clip(1.0 + 0.15 * jax.random.normal(streams_of[14], (D,), jnp.float32), 0.25, 1.75)
    return dict(tokens=tokens, positions=positions, cotangent=cotangent, live_count=live_count, qkv_weight=qkv_weight, out_weight=out_weight, gate_weight=gate_weight, up_weight=up_weight, down_weight=down_weight, gain_in=gain_in, gain_query=gain_query, gain_key=gain_key, gain_attn=gain_attn, gain_pre=gain_pre, gain_post=gain_post)


epsilon = 1e-06
rope_base = 1000000.0
score_scale = 0.0625
masked_score = -1e+30

def rms_norm(values, gain_vec):
    inv_rms = lax.rsqrt(lax.optimization_barrier(jnp.mean(values * values, axis=-1, keepdims=True)) + epsilon)
    return values * inv_rms * gain_vec

def norm_back(values, gain_vec, upstream):
    inv_rms = lax.rsqrt(lax.optimization_barrier(jnp.mean(values * values, axis=-1, keepdims=True)) + epsilon)
    unit_val = values * inv_rms
    gain_grad = lax.optimization_barrier(jnp.sum((upstream * unit_val).reshape(-1, values.shape[-1]), axis=0))
    inner_grad = upstream * gain_vec
    value_grad = inv_rms * (inner_grad - unit_val * lax.optimization_barrier(jnp.mean(inner_grad * unit_val, axis=-1, keepdims=True)))
    return (value_grad, gain_grad)

def rotary(pos_rows):
    half_dim = HD // 2
    frequency = rope_base ** (-(jnp.arange(half_dim, dtype=jnp.float32) * 2.0 / HD))
    angles = pos_rows.astype(jnp.float32)[:, None] * frequency[None, :]
    angles = jnp.concatenate([angles, angles], axis=1)
    return (jnp.cos(angles), jnp.sin(angles))

def rotate(values, cosine, sine):
    half_dim = values.shape[-1] // 2
    lower_half = values[..., :half_dim]
    upper_half = values[..., half_dim:]
    turned = jnp.concatenate([-upper_half, lower_half], axis=-1)
    return values * cosine + turned * sine

def gelu_tanh(values):
    return jax.nn.gelu(values, approximate=True)

def dot32(left, right):
    return jnp.dot(left, right, preferred_element_type=jnp.float32)

def layer(tokens, positions, cotangent, live_seq, qkv_weight, out_weight, gate_weight, up_weight, down_weight, gain_in, gain_query, gain_key, gain_attn, gain_pre, gain_post):
    seq_count, seq_len, model_width = tokens.shape
    token_rows = seq_count * seq_len
    inner_width = H * HD
    seq_index = jnp.arange(seq_len, dtype=jnp.int32)
    causal = seq_index[:, None] >= seq_index[None, :]
    inputs = tokens.reshape(token_rows, model_width).astype(jnp.float32)
    normed_in = rms_norm(inputs, gain_in).astype(jnp.bfloat16)
    projected = dot32(normed_in, qkv_weight)
    cosine, sine = rotary(positions.reshape(token_rows))
    query_pre = projected[:, :inner_width].reshape(token_rows, H, HD)
    key_pre = projected[:, inner_width:inner_width + HD]
    queries = rotate(rms_norm(query_pre, gain_query), cosine[:, None], sine[:, None]).astype(jnp.bfloat16)
    key_rows = rotate(rms_norm(key_pre, gain_key), cosine, sine).astype(jnp.bfloat16)
    value_rows = projected[:, inner_width + HD:].astype(jnp.bfloat16)
    query_blocks = queries.reshape(seq_count, seq_len, H, HD).astype(jnp.float32)
    key_blocks = key_rows.reshape(seq_count, seq_len, HD).astype(jnp.float32)
    value_blocks = value_rows.reshape(seq_count, seq_len, HD).astype(jnp.float32)
    raw_scores = jnp.einsum('sqhd,skd->shqk', query_blocks, key_blocks) * score_scale
    raw_scores = jnp.where(causal[None, None], raw_scores, masked_score)
    row_max = lax.optimization_barrier(jnp.max(raw_scores, axis=-1, keepdims=True))
    log_total = row_max + jnp.log(lax.optimization_barrier(jnp.sum(jnp.exp(raw_scores - row_max), axis=-1, keepdims=True)))
    probs = jnp.exp(raw_scores - log_total)
    probs_bf = probs.astype(jnp.bfloat16)
    mixed = jnp.einsum('shqk,skd->sqhd', probs_bf.astype(jnp.float32), value_blocks)
    mixed_bf = mixed.reshape(token_rows, inner_width).astype(jnp.bfloat16)
    attended = dot32(mixed_bf, out_weight)
    residual = inputs + rms_norm(attended, gain_attn)
    normed_pre = rms_norm(residual, gain_pre).astype(jnp.bfloat16)
    gate_pre = dot32(normed_pre, gate_weight)
    up_pre = dot32(normed_pre, up_weight)
    activated, gelu_back = jax.vjp(gelu_tanh, gate_pre)
    hidden = (activated * up_pre).astype(jnp.bfloat16)
    ffn_out = dot32(hidden, down_weight)
    output = residual + rms_norm(ffn_out, gain_post)
    live_rows = jnp.repeat(live_seq, seq_len)[:, None]
    upstream = cotangent.reshape(token_rows, model_width).astype(jnp.float32) * live_rows
    ffn_grad, post_grad = norm_back(ffn_out, gain_post, upstream)
    ffn_grad_bf = ffn_grad.astype(jnp.bfloat16)
    hidden_grad = dot32(ffn_grad_bf, down_weight.T)
    down_term = dot32(hidden.T, ffn_grad_bf)
    gate_grad_bf = gelu_back(hidden_grad * up_pre)[0].astype(jnp.bfloat16)
    up_grad_bf = (hidden_grad * activated).astype(jnp.bfloat16)
    gate_term = dot32(normed_pre.T, gate_grad_bf)
    up_term = dot32(normed_pre.T, up_grad_bf)
    pre_in_grad = dot32(gate_grad_bf, gate_weight.T) + dot32(up_grad_bf, up_weight.T)
    res_part, pre_grad = norm_back(residual, gain_pre, pre_in_grad)
    residual_grad = upstream + res_part
    attn_out_grad, attn_grad = norm_back(attended, gain_attn, residual_grad)
    attn_out_bf = attn_out_grad.astype(jnp.bfloat16)
    out_term = dot32(mixed_bf.T, attn_out_bf)
    mixed_grad = dot32(attn_out_bf, out_weight.T).astype(jnp.bfloat16)
    mixed_grad = mixed_grad.reshape(seq_count, seq_len, H, HD).astype(jnp.float32)
    prob_grad = jnp.einsum('sqhd,skd->shqk', mixed_grad, value_blocks)
    row_dot = lax.optimization_barrier(jnp.sum(probs * prob_grad, axis=-1, keepdims=True))
    score_grad = (probs * (prob_grad - row_dot) * score_scale).astype(jnp.bfloat16).astype(jnp.float32)
    value_grad = jnp.einsum('shqk,sqhd->skd', probs_bf.astype(jnp.float32), mixed_grad)
    query_grad = jnp.einsum('shqk,skd->sqhd', score_grad, key_blocks)
    key_grad = jnp.einsum('shqk,sqhd->skd', score_grad, query_blocks)
    query_unrot = rotate(query_grad.reshape(token_rows, H, HD), cosine[:, None], -sine[:, None])
    query_in, query_gain_grad = norm_back(query_pre, gain_query, query_unrot)
    key_unrot = rotate(key_grad.reshape(token_rows, HD), cosine, -sine)
    key_in, key_gain_grad = norm_back(key_pre, gain_key, key_unrot)
    packed_grad = jnp.concatenate([query_in.reshape(token_rows, inner_width), key_in, value_grad.reshape(token_rows, HD)], axis=1).astype(jnp.bfloat16)
    qkv_term = dot32(normed_in.T, packed_grad)
    normed_grad = dot32(packed_grad, qkv_weight.T)
    input_part, in_grad = norm_back(inputs, gain_in, normed_grad)
    input_grad = residual_grad + input_part
    terms = (qkv_term, out_term, gate_term, up_term, down_term)
    gain_terms = (in_grad, query_gain_grad, key_gain_grad, attn_grad, pre_grad, post_grad)
    return (output.reshape(seq_count, seq_len, model_width), input_grad.reshape(seq_count, seq_len, model_width), terms, gain_terms)

def reference(tokens, positions, cotangent, live_count, qkv_weight, out_weight, gate_weight, up_weight, down_weight, gain_in, gain_query, gain_key, gain_attn, gain_pre, gain_post):
    seq_total = tokens.shape[0]
    group_size = math.gcd(seq_total, 16)
    block_count = seq_total // group_size
    seq_ids = jnp.arange(seq_total, dtype=jnp.int32)
    live_seq = (seq_ids % SLOTS < live_count[seq_ids // SLOTS]).astype(jnp.float32)
    blocks = (tokens.reshape(block_count, group_size, LEN, D), positions.reshape(block_count, group_size, LEN), cotangent.reshape(block_count, group_size, LEN, D), live_seq.reshape(block_count, group_size))
    weights = (qkv_weight, out_weight, gate_weight, up_weight, down_weight)
    gains = (gain_in, gain_query, gain_key, gain_attn, gain_pre, gain_post)
    start = (tuple((jnp.zeros(w.shape, jnp.float32) for w in weights)), tuple((jnp.zeros(g.shape, jnp.float32) for g in gains)))

    def step(carry, block_in):
        output, input_grad, terms, gain_terms = layer(block_in[0], block_in[1], block_in[2], block_in[3], qkv_weight, out_weight, gate_weight, up_weight, down_weight, gain_in, gain_query, gain_key, gain_attn, gain_pre, gain_post)
        carry = jax.tree.map(lambda left, right: left + right, carry, (terms, gain_terms))
        return (carry, (output, input_grad))
    (terms, gain_terms), (outputs, input_grads) = lax.scan(step, start, blocks)
    output = outputs.reshape(seq_total, LEN, D)
    input_grad = input_grads.reshape(seq_total, LEN, D)
    return (output, input_grad, terms[0], terms[1], terms[2], terms[3], terms[4], gain_terms[0], gain_terms[1], gain_terms[2], gain_terms[3], gain_terms[4], gain_terms[5])
```

```python
import jax
import jax.numpy as jnp
from jax import lax
from jax.sharding import PartitionSpec as P

H = 4
HD = 256


epsilon = 1e-06
rope_base = 1000000.0
score_scale = 0.0625
masked_score = -1e30


def rms_norm(values, gain_vec):
    inv_rms = lax.rsqrt(jnp.mean(values * values, axis=-1, keepdims=True) + epsilon)
    return values * inv_rms * gain_vec


def norm_back(values, gain_vec, upstream):
    inv_rms = lax.rsqrt(jnp.mean(values * values, axis=-1, keepdims=True) + epsilon)
    unit_val = values * inv_rms
    gain_grad = jnp.sum((upstream * unit_val).reshape(-1, values.shape[-1]), axis=0)
    inner_grad = upstream * gain_vec
    value_grad = inv_rms * (
        inner_grad - unit_val * jnp.mean(inner_grad * unit_val, axis=-1, keepdims=True)
    )
    return (value_grad, gain_grad)


def rotary(pos_rows):
    half_dim = HD // 2
    frequency = rope_base ** (-(jnp.arange(half_dim, dtype=jnp.float32) * 2.0 / HD))
    angles = pos_rows.astype(jnp.float32)[:, None] * frequency[None, :]
    angles = jnp.concatenate([angles, angles], axis=1)
    return (jnp.cos(angles), jnp.sin(angles))


def rotate(values, cosine, sine):
    half_dim = values.shape[-1] // 2
    lower_half = values[..., :half_dim]
    upper_half = values[..., half_dim:]
    turned = jnp.concatenate([-upper_half, lower_half], axis=-1)
    return values * cosine + turned * sine


def gelu_tanh(values):
    return jax.nn.gelu(values, approximate=True)


def dot32(left, right):
    return jnp.dot(left, right, preferred_element_type=jnp.float32)


def masked_scores(query_blocks, key_blocks, causal):
    raw_scores = (
        jnp.einsum("sqhd,skd->shqk", query_blocks, key_blocks, preferred_element_type=jnp.float32)
        * score_scale
    )
    return jnp.where(causal[None, None], raw_scores, masked_score)


def swap(values, axis, bit):
    count = lax.axis_size(axis)
    return lax.ppermute(values, axis, [(i, i ^ bit) for i in range(count)])


def rounded(values):
    return values.astype(jnp.bfloat16)


def spread(block):
    far = swap(block, "shard", 2)
    side = swap(jnp.stack([block, far]), "shard", 1)
    return [block, side[0], far, side[1]]


def spread_weight(block, row_bit, pieces):
    rows, cols = block.shape
    half = rows // 2
    step = half // pieces
    shard_idx = lax.axis_index("shard")
    mine = lax.dynamic_slice_in_dim(block, row_bit * half, half, 0)
    full = jnp.zeros((lax.axis_size("shard") * rows, cols), block.dtype)
    near = [mine[i * step : (i + 1) * step] for i in range(pieces)]
    far = [swap(piece, "shard", 2) for piece in near]
    relayed = [swap(piece, "replica", 1) for piece in far]
    other = jnp.zeros_like(block)
    for i in range(pieces):
        other = lax.dynamic_update_slice_in_dim(other, far[i], row_bit * half + i * step, 0)
        other = lax.dynamic_update_slice_in_dim(other, relayed[i], (1 - row_bit) * half + i * step, 0)
    side_own = swap(block, "shard", 1)
    side_other = swap(other, "shard", 1)
    for k, part in enumerate((block, side_own, other, side_other)):
        full = lax.dynamic_update_slice_in_dim(full, part, (shard_idx ^ k) * rows, 0)
    return full


def column_quarter(weight, row_bit):
    rows, cols = weight.shape
    count = lax.axis_size("shard")
    width = cols // count
    half = rows // 2
    shard_idx = lax.axis_index("shard")
    stacked = jnp.stack([weight[:, j * width : (j + 1) * width] for j in range(count)])
    take = lambda k: lax.dynamic_index_in_dim(stacked, shard_idx ^ k, 0, keepdims=False)
    full = jnp.zeros((count * rows, width), weight.dtype)
    put = lambda full, part, start: lax.dynamic_update_slice_in_dim(full, part, start, 0)
    for k in (2, 3):
        piece = lax.dynamic_slice_in_dim(take(k), row_bit * half, half, 0)
        far = swap(piece, "shard", k)
        relayed = swap(far, "replica", 1)
        full = put(full, far, (shard_idx ^ k) * rows + row_bit * half)
        full = put(full, relayed, (shard_idx ^ k) * rows + (1 - row_bit) * half)
    full = put(full, take(0), shard_idx * rows)
    return put(full, swap(take(1), "shard", 1), (shard_idx ^ 1) * rows)


def sum_shards(parts):
    side = swap(jnp.stack([parts[1], parts[3]]), "shard", 1)
    own = parts[0] + side[0]
    far = parts[2] + side[1]
    return own + swap(rounded(far), "shard", 2).astype(jnp.float32)


def halve(blocks, bit, index_bit):
    keep = [k for k in blocks if not k & index_bit]
    sent = swap(jnp.stack([blocks[k | index_bit] for k in keep]), "replica", bit)
    return {
        k: rounded(blocks[k].astype(jnp.float32) + sent[i].astype(jnp.float32))
        if len(keep) > 1
        else blocks[k].astype(jnp.float32) + sent[i].astype(jnp.float32)
        for i, k in enumerate(keep)
    }


def bits_of(count):
    return [1 << i for i in range(count.bit_length() - 1)]


def reduce_blocks(blocks, order):
    for bit in order:
        blocks = halve(blocks, bit, bit)
    return blocks[0]


def shards(
    tokens,
    positions,
    cotangent,
    live_count,
    qkv_weight,
    out_weight,
    gate_weight,
    up_weight,
    down_weight,
    gain_in,
    gain_query,
    gain_key,
    gain_attn,
    gain_pre,
    gain_post,
):
    slot_count, block_len, model_width = tokens.shape
    token_rows = slot_count * block_len
    inner_width = H * HD
    shard_idx = lax.axis_index("shard")
    shard_count = lax.axis_size("shard")
    group_idx = lax.axis_index("replica")
    group_count = lax.axis_size("replica")
    row_bit = group_idx % 2
    query_index = shard_idx * block_len + jnp.arange(block_len, dtype=jnp.int32)
    key_index = jnp.concatenate(
        [(shard_idx ^ k) * block_len + jnp.arange(block_len, dtype=jnp.int32) for k in range(shard_count)]
    )
    causal = query_index[:, None] >= key_index[None, :]
    attn_full = spread_weight(qkv_weight, row_bit, 2)
    proj_full = spread_weight(out_weight, row_bit, 1)
    gate_cols = column_quarter(gate_weight, row_bit)
    up_cols = column_quarter(up_weight, row_bit)
    inputs = tokens.reshape(token_rows, model_width).astype(jnp.float32)
    normed_in = rms_norm(inputs, gain_in).astype(jnp.bfloat16)
    projected = dot32(normed_in, attn_full)
    cosine, sine = rotary(positions.reshape(token_rows))
    query_pre = projected[:, :inner_width].reshape(token_rows, H, HD)
    key_pre = projected[:, inner_width : inner_width + HD]
    queries = rotate(rms_norm(query_pre, gain_query), cosine[:, None], sine[:, None]).astype(
        jnp.bfloat16
    )
    key_local = rotate(rms_norm(key_pre, gain_key), cosine, sine).astype(jnp.bfloat16)
    value_local = projected[:, inner_width + HD :].astype(jnp.bfloat16)
    pair_local = jnp.stack([key_local, value_local]).reshape(2, slot_count, block_len, HD)
    pair_blocks = jnp.concatenate(spread(pair_local), axis=2)
    key_blocks, value_blocks = (pair_blocks[0], pair_blocks[1])
    query_blocks = queries.reshape(slot_count, block_len, H, HD)
    raw_scores = masked_scores(query_blocks, key_blocks, causal)
    row_max = jnp.max(raw_scores, axis=-1, keepdims=True)
    log_total = row_max + jnp.log(jnp.sum(jnp.exp(raw_scores - row_max), axis=-1, keepdims=True))
    probs = jnp.exp(raw_scores - log_total)
    probs_bf = probs.astype(jnp.bfloat16)
    mixed = jnp.einsum("shqk,skd->sqhd", probs_bf, value_blocks, preferred_element_type=jnp.float32)
    mixed_bf = mixed.reshape(token_rows, inner_width).astype(jnp.bfloat16)
    attended = dot32(mixed_bf, proj_full)
    residual = inputs + rms_norm(attended, gain_attn)
    normed_pre = rms_norm(residual, gain_pre).astype(jnp.bfloat16)
    pre_group = jnp.concatenate(spread(normed_pre), axis=0)
    gate_pre = dot32(pre_group, gate_cols)
    up_pre = dot32(pre_group, up_cols)
    activated, gelu_back = jax.vjp(gelu_tanh, gate_pre)
    hidden = (activated * up_pre).astype(jnp.bfloat16)
    ffn_parts = dot32(hidden, down_weight).reshape(shard_count, token_rows, model_width)
    ffn_out = sum_shards(ffn_parts)
    output = residual + rms_norm(ffn_out, gain_post)
    live_slots = (jnp.arange(slot_count, dtype=jnp.int32) < live_count[0]).astype(jnp.float32)
    live_rows = jnp.repeat(live_slots, block_len)[:, None]
    upstream = cotangent.reshape(token_rows, model_width).astype(jnp.float32) * live_rows
    ffn_grad, post_grad = norm_back(ffn_out, gain_post, upstream)
    ffn_group = jnp.concatenate(spread(ffn_grad.astype(jnp.bfloat16)), axis=0)
    hidden_grad = dot32(ffn_group, down_weight.T)
    gate_grad_bf = gelu_back(hidden_grad * up_pre)[0].astype(jnp.bfloat16)
    up_grad_bf = (hidden_grad * activated).astype(jnp.bfloat16)

    ffn_rows = ffn_group.T.reshape(group_count, model_width // group_count, -1)
    ffn_rows = ffn_rows[jnp.arange(group_count) ^ group_idx].reshape(model_width, -1)
    down_blocks = rounded(dot32(ffn_rows, hidden)).reshape(
        group_count, model_width // group_count, -1
    )
    low_count = group_count // shard_count
    all_bits = bits_of(group_count)
    low_bits = bits_of(low_count)[::-1]
    high_bits = [b for b in all_bits if b >= low_count]
    down_order = high_bits[:1] + low_bits + high_bits[1:]
    down_sum = reduce_blocks(dict(enumerate(down_blocks)), down_order).T

    low_idx = group_idx % low_count
    high_idx = group_idx // low_count
    pre_rows = pre_group.T.reshape(shard_count, model_width // shard_count, -1)
    pre_rows = pre_rows[jnp.arange(shard_count) ^ shard_idx].reshape(model_width, -1)

    def owned_sum(grad):
        width = grad.shape[1] // low_count
        cols = jnp.stack([grad[:, b * width : (b + 1) * width] for b in range(low_count)])
        blocks = {
            k: rounded(
                dot32(pre_rows, lax.dynamic_index_in_dim(cols, low_idx ^ k, 0, keepdims=False))
            ).reshape(shard_count, -1, width)
            for k in range(low_count)
        }
        for bit in low_bits:
            keep = [k for k in blocks if not k & bit]
            blocks = {
                k: rounded(
                    blocks[k].astype(jnp.float32)
                    + swap(blocks[k | bit], "replica", bit).astype(jnp.float32)
                )
                for k in keep
            }
        mine = blocks[0]
        moved = jnp.stack([mine[0]] + [swap(mine[k], "shard", k) for k in range(1, shard_count)])
        turn = high_idx ^ shard_idx
        ordered = {
            m: lax.dynamic_index_in_dim(moved, turn ^ m, 0, keepdims=False)
            for m in range(shard_count)
        }
        for bit in high_bits:
            ordered = halve(ordered, bit, bit // low_count)
        return ordered[0]

    gate_sum = owned_sum(gate_grad_bf)
    up_sum = owned_sum(up_grad_bf)

    pre_parts = dot32(gate_grad_bf, gate_cols.T) + dot32(up_grad_bf, up_cols.T)
    pre_in_grad = sum_shards(pre_parts.reshape(shard_count, token_rows, model_width))
    res_part, pre_grad = norm_back(residual, gain_pre, pre_in_grad)
    residual_grad = upstream + res_part
    attn_out_grad, attn_grad = norm_back(attended, gain_attn, residual_grad)
    attn_out_bf = attn_out_grad.astype(jnp.bfloat16)
    mixed_grad = (
        dot32(attn_out_bf, proj_full.T).astype(jnp.bfloat16).reshape(slot_count, block_len, H, HD)
    )
    prob_grad = jnp.einsum(
        "sqhd,skd->shqk", mixed_grad, value_blocks, preferred_element_type=jnp.float32
    )
    row_dot = jnp.sum(probs * prob_grad, axis=-1, keepdims=True)
    score_grad = (probs * (prob_grad - row_dot) * score_scale).astype(jnp.bfloat16)
    value_part = jnp.einsum(
        "shqk,sqhd->skd", probs_bf, mixed_grad, preferred_element_type=jnp.float32
    )
    query_grad = jnp.einsum(
        "shqk,skd->sqhd", score_grad, key_blocks, preferred_element_type=jnp.float32
    )
    key_part = jnp.einsum(
        "shqk,sqhd->skd", score_grad, query_blocks, preferred_element_type=jnp.float32
    )
    pair_part = jnp.stack([key_part, value_part])
    pair_grad = sum_shards(
        [pair_part[:, :, k * block_len : (k + 1) * block_len] for k in range(shard_count)]
    )
    key_grad, value_grad = (pair_grad[0], pair_grad[1])
    query_unrot = rotate(query_grad.reshape(token_rows, H, HD), cosine[:, None], -sine[:, None])
    query_in, query_gain_grad = norm_back(query_pre, gain_query, query_unrot)
    key_unrot = rotate(key_grad.reshape(token_rows, HD), cosine, -sine)
    key_in, key_gain_grad = norm_back(key_pre, gain_key, key_unrot)
    packed_grad = jnp.concatenate(
        [query_in.reshape(token_rows, inner_width), key_in, value_grad.reshape(token_rows, HD)],
        axis=1,
    ).astype(jnp.bfloat16)
    normed_grad = dot32(packed_grad, attn_full.T)
    input_part, in_grad = norm_back(inputs, gain_in, normed_grad)
    input_grad = residual_grad + input_part

    def own_columns(values):
        width = values.shape[1] // shard_count
        cols = jnp.stack([values[:, j * width : (j + 1) * width] for j in range(shard_count)])
        parts = [
            lax.dynamic_index_in_dim(cols, shard_idx ^ k, 0, keepdims=False)
            for k in range(shard_count)
        ]
        return jnp.concatenate(
            [parts[0]] + [swap(parts[k], "shard", k) for k in range(1, shard_count)], axis=0
        )

    def group_sum(owned, grads, order):
        rows = grads.T.reshape(group_count, grads.shape[1] // group_count, -1)
        rows = rows[jnp.arange(group_count) ^ group_idx].reshape(grads.shape[1], -1)
        blocks = rounded(dot32(rows, owned)).reshape(group_count, -1, owned.shape[1])
        return reduce_blocks(dict(enumerate(blocks)), order).T

    order = low_bits + high_bits
    out_sum = group_sum(
        own_columns(mixed_bf), jnp.concatenate(spread(attn_out_bf), axis=0), order
    )
    qkv_sum = group_sum(
        own_columns(normed_in), jnp.concatenate(spread(packed_grad), axis=0), order
    )

    gains = jnp.concatenate(
        [in_grad, query_gain_grad, key_gain_grad, attn_grad, pre_grad, post_grad]
    )
    for bit in bits_of(shard_count):
        gains = gains + swap(gains, "shard", bit)
    for bit in all_bits:
        gains = gains + swap(gains, "replica", bit)
    gain_sums = []
    start = 0
    for grad in (in_grad, query_gain_grad, key_gain_grad, attn_grad, pre_grad, post_grad):
        gain_sums.append(gains[start : start + grad.shape[0]])
        start += grad.shape[0]
    return (
        output.reshape(slot_count, block_len, model_width),
        input_grad.reshape(slot_count, block_len, model_width),
        qkv_sum,
        out_sum,
        gate_sum,
        up_sum,
        down_sum,
        *gain_sums,
    )


def solution(mesh):
    in_specs = (
        P("replica", "shard", None),
        P("replica", "shard"),
        P("replica", "shard", None),
        P("replica"),
        P("shard", None),
        P("shard", None),
        P("shard", None),
        P("shard", None),
        P("shard", None),
        P(),
        P(),
        P(),
        P(),
        P(),
        P(),
    )
    out_specs = (
        P("replica", "shard", None),
        P("replica", "shard", None),
        P("shard", "replica"),
        P("shard", "replica"),
        P("shard", "replica"),
        P("shard", "replica"),
        P("shard", "replica"),
        P(),
        P(),
        P(),
        P(),
        P(),
        P(),
    )
    return jax.shard_map(shards, mesh=mesh, in_specs=in_specs, out_specs=out_specs, check_vma=False)
```
